32 devices in a mesh: tm: 2 (over y), obs: 16 (over z, x, core).
Axes of the slice: x: 2, y: 2, z: 4, core: 2. Of those that a mesh axis runs over, the one named last changes fastest.
Arguments:
- flux: bfloat16 [4, 64, 16384], P('tm', 'obs'), may hold values from -6 to 6
- footprint: bfloat16 [2048, 16384], P(('tm', 'obs')), may hold values from -0.046875 to 0.046875
- entry_owner: int32 [2048, 1], P(('tm', 'obs')), may hold values from 0 to 15; in each aligned block of 64 rows (0 to 63, 64 to 127, ...) at most 8 rows name the same one
- entry_tile: int32 [32, 64], P(('tm', 'obs')), may hold values from 0 to 3
- entry_lag: int32 [32, 64], P(('tm', 'obs')), may hold values from 0 to 1
- entry_sounding: int32 [32, 64], P(('tm', 'obs')), may hold values from 0 to 15, never falling along the last dimension, each value on 1 to 8 neighbouring positions
- sounding_window: int32 [32, 16], P(('tm', 'obs')), may hold values from 1 to 3
- observed: float32 [32, 16], P(('tm', 'obs')), may hold values from -8 to 8
- obs_weight: float32 [32, 16], P(('tm', 'obs')), may hold values from 0.25 to 4
Outputs:
- modeled: float32 [32, 16], P(('tm', 'obs'))
- gradient: float32 [4, 64, 16384], P('tm', 'obs')
The draws below stay inside these ranges and needn't reach their ends.
Inputs may be any that keep to these rules, and one draw needn't show every extreme that they name: `entry_owner`: among the 64 entries of one device no owner is named more than 8 times, and on some device some owner is named exactly 8 times.
All inputs are finite; a program needn't handle non-finite values.
Results may differ from the reference program's by a relative error of at most 0.0029.
Values may be sent and summed in bfloat16 or wider, within the bound.
A program may use at most 64 MiB of HBM per device.

```python
import math
import jax
import jax.numpy as jnp
import numpy as np
from jax import lax

CELLS = 16384
E_DEV = 64
TILE_DEV = 4
S_DEV = 16
WIN = 4
TILES = 64
LAGS = 2
CAP = 8
N_OBS = 16
DEVICES = 32


def plant(result, own_key, smallest, top_value):
    place = [jax.random.randint(jax.random.fold_in(own_key, axis), (), 0, length) for axis, length in enumerate(result.shape)]
    main_axis = result.shape.index(max(result.shape))
    beside = place[:main_axis] + [(place[main_axis] + 1) % result.shape[main_axis]] + place[main_axis + 1:]
    return result.at[tuple(place)].set(smallest).at[tuple(beside)].set(top_value)


def shard_levels(key, shape, cuts, low, largest):
    factor_of = 1.0
    for axis_at, parts in cuts:
        heights = jax.random.uniform(jax.random.fold_in(jax.random.fold_in(key, 6), axis_at), (parts,), jnp.float32, low / len(cuts), largest / len(cuts))
        factor_of = factor_of * jnp.repeat(jnp.exp(heights), shape[axis_at] // parts).reshape((-1,) + (1,) * (len(shape) - 1 - axis_at))
    return factor_of


def split_up(count, total, limit, lean):
    loads = [(1 << 20) // math.isqrt(grade ** lean) + 1 for grade in range(2, count + 1)]
    rest, counts = total - limit - (count - 1), [1] * (count - 1)
    while rest > 0:
        candidates = [i for i in range(count - 1) if counts[i] < limit]
        mass, remaining = sum([loads[i] for i in candidates]), rest
        for i in candidates:
            extra = min(limit - counts[i], max(1, remaining * loads[i] // mass), rest)
            counts[i] = counts[i] + extra
            rest = rest - extra
    return np.array([limit] + counts)


def ragged_sizes(stream_key, count, total, most, slope):
    if count == 2:
        one = jax.random.randint(stream_key, (), max(1, total - most), min(most, total - 1) + 1)
        return jnp.stack([one, total - one])
    lengths = jnp.asarray(split_up(count, total, most, slope), jnp.int32)
    couples = (count - 1) // 2
    giver, receiver = lengths[1:1 + 2 * couples:2], lengths[2:2 + 2 * couples:2]
    room = jnp.minimum(giver - 1, most - receiver)
    moved = jax.random.randint(jax.random.fold_in(stream_key, 1), (couples,), 0, 1 << 20) % (room + 1)
    lengths = lengths.at[1:1 + 2 * couples:2].set(giver - moved).at[2:2 + 2 * couples:2].set(receiver + moved)
    return lengths[jax.random.permutation(jax.random.fold_in(stream_key, 2), count)]


def routed_block(key, own, number, rows, amount, top, most, lean):
    order = jax.random.permutation(key, amount)
    crowded, common = shares(amount, rows * top, most, lean, True), shares(amount, rows * top, most, lean, False)
    places = jnp.arange(amount)

    def named(sizes, offset_by):
        used = int((sizes > 0).sum())
        fixed = max(1, used // 4)
        shifted = fixed + (places - fixed + offset_by * (used - fixed)) % max(1, amount - fixed)
        return jnp.zeros((amount,), jnp.int32).at[order[jnp.where(places < fixed, places, shifted)]].set(jnp.asarray(sizes, jnp.int32))

    sizes = jnp.where(number % 4 == 0, named(crowded, number // 4), named(common, number - number // 4 - 1))
    mixed = jax.random.permutation(jax.random.fold_in(own, 3), amount)
    donor, taker = mixed[0:amount // 2 * 2:2], mixed[1:amount // 2 * 2:2]
    margin = jnp.minimum(sizes[donor] - 1, most - sizes[taker]) // 2
    margin = jnp.where((donor == order[0]) | (taker == order[0]) | (sizes[taker] == 0), 0, jnp.maximum(margin, 0))
    shifted = jax.random.randint(jax.random.fold_in(own, 4), (amount // 2,), 0, 1 << 20) % (margin + 1)
    sizes = sizes.at[donor].add(-shifted).at[taker].add(shifted)
    labels = jnp.searchsorted(jnp.cumsum(sizes), jnp.arange(rows * top), side="right").astype(jnp.int32)
    table = labels.reshape(top, rows).T
    table = table[jax.random.permutation(jax.random.fold_in(own, 1), rows)]
    offset_by = jax.random.randint(jax.random.fold_in(own, 2), (rows, 1), 0, top)
    return jnp.take_along_axis(table, (jnp.arange(top)[None, :] + offset_by) % top, axis=1)


def shares(count, total, limit, slope, full):
    loads = [(1 << 20) // math.isqrt(grade ** slope) + 1 for grade in range(1, count + 1)]
    largest = limit if full else min(limit, max(-(-total // count), total * loads[0] // sum(loads)))
    least = 1 if total - largest >= count - 1 else 0
    given, rest = [largest] + [least] * (count - 1), total - largest - least * (count - 1)
    while rest > 0:
        candidates = [i for i in range(1, count) if given[i] < largest] or [i for i in range(1, count) if given[i] < limit]
        pool, left = sum([loads[i] for i in candidates]), rest
        for i in candidates:
            extra = min(limit - given[i], max(1, left * loads[i] // pool), rest)
            given[i] = given[i] + extra
            rest = rest - extra
    return np.array(given)


def gaussian(rng, shape, scale, most, pieces=(), kind=jnp.bfloat16):
    drawn = scale * jax.random.normal(rng, shape, jnp.float32)
    if pieces:
        drawn = drawn * shard_levels(rng, shape, pieces, -0.22, 0.18)
    return jnp.clip(drawn, -most, most).astype(kind)


def setup_inputs(seed: int = 0) -> dict:
    arg_keys = jax.random.split(jax.random.key(seed), 10)
    flux = gaussian(arg_keys[0], (WIN, TILES, CELLS), 1.0, 6.0, ((0, 2), (1, 16)))
    footprint = gaussian(arg_keys[1], (DEVICES * E_DEV, CELLS), CELLS ** -0.5, 0.046875, ((0, 32),))
    entry_owner_keys = jax.random.split(jax.random.fold_in(arg_keys[2], 1), (DEVICES * E_DEV) // E_DEV)
    entry_owner_turns = jax.random.permutation(jax.random.fold_in(arg_keys[2], 3), (DEVICES * E_DEV) // E_DEV)
    entry_owner = jax.vmap(lambda own, number: routed_block(jax.random.fold_in(arg_keys[2], 2), own, number, E_DEV, N_OBS, 1, CAP, 2))(entry_owner_keys, entry_owner_turns).reshape((DEVICES * E_DEV, 1))
    entry_tile = plant(jax.random.randint(arg_keys[3], (DEVICES, E_DEV), 0, TILE_DEV), jax.random.fold_in(arg_keys[3], 1), 0, TILE_DEV - 1).astype(jnp.int32)
    entry_lag = plant(jax.random.randint(arg_keys[4], (DEVICES, E_DEV), 0, LAGS), jax.random.fold_in(arg_keys[4], 1), 0, LAGS - 1).astype(jnp.int32)
    entry_sounding = jax.vmap(lambda own: jnp.searchsorted(jnp.cumsum(ragged_sizes(own, S_DEV, E_DEV, 8, 1)), jnp.arange(E_DEV), side="right"))(jax.random.split(arg_keys[5], DEVICES)).reshape((DEVICES, E_DEV)).astype(jnp.int32)
    sounding_window = plant(jax.random.randint(arg_keys[6], (DEVICES, S_DEV), LAGS - 1, WIN), jax.random.fold_in(arg_keys[6], 1), LAGS - 1, WIN - 1).astype(jnp.int32)
    observed = gaussian(arg_keys[7], (DEVICES, S_DEV), 2.0, 8.0, ((0, 32),), jnp.float32)
    obs_weight = jnp.clip(jnp.exp(math.log(4.0) - 2.7725887 * jax.random.uniform(arg_keys[8], (DEVICES, S_DEV), jnp.float32) ** shard_levels(arg_keys[8], (DEVICES, S_DEV), ((0, 32),), -0.2, 0.2)), 0.25, 4.0)
    return {"flux": flux, "footprint": footprint, "entry_owner": entry_owner, "entry_tile": entry_tile, "entry_lag": entry_lag, "entry_sounding": entry_sounding, "sounding_window": sounding_window, "observed": observed, "obs_weight": obs_weight}


def reference(flux, footprint, entry_owner, entry_tile, entry_lag, entry_sounding, sounding_window, observed, obs_weight):
    flat_flux = flux.reshape(WIN * TILES, CELLS)
    blocks = footprint.reshape(DEVICES, E_DEV, CELLS)
    owners = entry_owner.reshape(DEVICES, E_DEV)
    window = jnp.take_along_axis(sounding_window, entry_sounding, axis=1) - entry_lag
    row_ids = (window * TILES + owners * TILE_DEV + entry_tile).astype(jnp.int32)

    def forward(inputs):
        block_rows, row_index = inputs
        selected = flat_flux[row_index]
        return jnp.sum(block_rows.astype(jnp.float32) * selected.astype(jnp.float32), axis=1)

    entry_dots = lax.map(forward, (blocks, row_ids))
    onehot = (entry_sounding[:, :, None] == jnp.arange(S_DEV, dtype=jnp.int32)[None, None, :]).astype(jnp.float32)
    modeled = jnp.sum(entry_dots[:, :, None] * onehot, axis=1)
    residual = obs_weight * (modeled - observed)
    entry_resid = jnp.take_along_axis(residual, entry_sounding, axis=1)

    def accumulate(running, inputs):
        block_rows, row_index, resid_rows = inputs
        contribution = (resid_rows[:, None] * block_rows.astype(jnp.float32)).astype(jnp.bfloat16).astype(jnp.float32)
        return running.at[row_index].add(contribution), None

    gradient, _ = lax.scan(accumulate, jnp.zeros((WIN * TILES, CELLS), jnp.float32), (blocks, row_ids, entry_resid))
    return modeled, gradient.reshape(WIN, TILES, CELLS)
```

```python
import functools

import jax
import jax.numpy as jnp
from jax import lax
from jax.experimental import pallas as pl
from jax.experimental.pallas import tpu as pltpu
from jax.sharding import PartitionSpec as P


def per_device(
    flux,
    footprint,
    entry_owner,
    entry_tile,
    entry_lag,
    entry_sounding,
    sounding_window,
    observed,
    obs_weight,
):
    peer_count = lax.axis_size("obs")
    entry_count = footprint.shape[0]
    cell_count = footprint.shape[1]
    tile_dev = flux.shape[1]
    sounding_count = observed.shape[1]
    slot_cap = 2 * entry_count // peer_count
    owners = entry_owner[:, 0]
    sounding = entry_sounding[0]
    sounding_hot = sounding[:, None] == jnp.arange(sounding_count, dtype=jnp.int32)[None, :]
    window = jnp.sum(jnp.where(sounding_hot, sounding_window[0][None, :], 0), axis=1) - entry_lag[0]
    target = window * tile_dev + entry_tile[0]
    owner_hot = (owners[:, None] == jnp.arange(peer_count, dtype=jnp.int32)[None, :]).astype(
        jnp.int32
    )
    rank_within = jnp.sum((jnp.cumsum(owner_hot, axis=0) - owner_hot) * owner_hot, axis=1)
    slot_index = owners * slot_cap + rank_within
    send_blocks = (
        jnp.zeros((peer_count * slot_cap, cell_count), jnp.bfloat16).at[slot_index].set(footprint)
    )
    send_blocks = send_blocks.reshape(peer_count, slot_cap, cell_count)
    send_target = jnp.zeros((peer_count * slot_cap,), jnp.int32).at[slot_index].set(target)
    send_target = send_target.reshape(peer_count, slot_cap)
    everything = lax.all_gather(flux, "tm", axis=0, tiled=True).reshape(-1, cell_count)
    got_blocks, got_target = (
        lax.all_to_all(send_blocks, "obs", split_axis=0, concat_axis=0, tiled=True),
        lax.all_to_all(send_target, "obs", split_axis=0, concat_axis=0, tiled=True),
    )
    selected = everything[got_target.reshape(-1)].reshape(got_blocks.shape)
    returned = lax.all_to_all(
        jnp.einsum("pkc,pkc->pk", got_blocks, selected, preferred_element_type=jnp.float32),
        "obs",
        split_axis=0,
        concat_axis=0,
        tiled=True,
    )
    entry_dots = returned.reshape(-1)[slot_index]
    modeled = jnp.sum(jnp.where(sounding_hot, entry_dots[:, None], 0.0), axis=0)
    residual = obs_weight[0] * (modeled - observed[0])
    entry_resid = jnp.sum(jnp.where(sounding_hot, residual[None, :], 0.0), axis=1)
    slot_resid = jnp.zeros((peer_count * slot_cap,), jnp.float32).at[slot_index].set(entry_resid)
    got_resid = lax.all_to_all(
        slot_resid.reshape(peer_count, slot_cap), "obs", split_axis=0, concat_axis=0, tiled=True
    )
    contribution = (got_resid[:, :, None] * got_blocks).astype(jnp.bfloat16)
    targets = got_target
    contribution = contribution.reshape(-1, cell_count)
    targets = targets.reshape(-1)
    row_count = flux.shape[0] * lax.axis_size("tm")
    row_ids = jnp.arange(row_count * tile_dev, dtype=jnp.int32)
    row_match = (row_ids[:, None] == targets[None, :]).astype(jnp.bfloat16)
    summed = jnp.dot(row_match, contribution, preferred_element_type=jnp.float32)
    gradient = lax.psum_scatter(
        summed.reshape(row_count, tile_dev * cell_count), "tm", scatter_dimension=0, tiled=True
    )
    gradient = gradient.reshape(flux.shape[0], tile_dev, cell_count)
    return (modeled[None, :], gradient)


KINDS = (
    "foot", "flux", "m0", "m1", "m2", "m3", "m4", "m5", "m6", "vals",
    "gup", "gdown", "g1x", "g1y", "g2x", "g2y",
    "s1x", "s1y", "s2x", "s2y", "up0", "up1", "down0", "down1", "fin",
)
KIND = {name: at for at, name in enumerate(KINDS)}


def eye(n):
    return lax.broadcasted_iota(jnp.int32, (n, n), 0) == lax.broadcasted_iota(jnp.int32, (n, n), 1)


def to_col(row):
    return jnp.sum(jnp.where(eye(row.shape[1]), row, 0.0), axis=1, keepdims=True)


def to_row(col):
    return jnp.sum(jnp.where(eye(col.shape[0]), col, 0.0), axis=0, keepdims=True)


def chip_kernel(
    depth, windows, tile_dev, flux, foot, owner, tile, lag, sounding, swin, observed, weight,
    modeled_out, out,
    foot_all, contrib, gath, owner_p, tile_p, lag_p, sounding_p, swin_p, observed_p, weight_p,
    val_send, val_recv, row_ids, t1x, t1y, a1x, a1y, t2x, t2y, a2x, a2y, zsum, zup, zdown,
    send_sem, recv_sem, local_sem,
):
    entries = foot.shape[0]
    half = foot.shape[1] // 2
    quarter = half // 2
    rows_dev = flux.shape[0]
    rows_chip = 2 * rows_dev
    rows_plane = 4 * rows_chip
    tile_cells = min(1024, quarter)
    tile_back = min(512, quarter)
    y = lax.axis_index("tm")
    o = lax.axis_index("obs")
    core = lax.rem(o, 2)
    x = lax.rem(o // 2, 2)
    z = o // 4
    partner = (y, o + 1 - 2 * core)
    xn = (y, o + 2 - 4 * x)
    yn = (1 - y, o)
    zu = (y, o + 4)
    zd = (y, o - 4)
    has_up = z < depth - 1
    has_down = z > 0

    def signal(device):
        pl.semaphore_signal(
            barrier, inc=1, device_id=device, device_id_type=pl.DeviceIdType.MESH
        )

    barrier = pltpu.get_barrier_semaphore()
    for device in (partner, xn, yn):
        signal(device)
    pl.when(has_up)(lambda: signal(zu))
    pl.when(has_down)(lambda: signal(zd))
    peers = 3 + jnp.where(has_up, 1, 0) + jnp.where(has_down, 1, 0)
    pl.semaphore_wait(barrier, peers)

    def remote(kind, at, src, dst, device):
        return pltpu.make_async_remote_copy(
            src_ref=src,
            dst_ref=dst,
            send_sem=send_sem.at[KIND[kind], at],
            recv_sem=recv_sem.at[KIND[kind], at],
            device_id=device,
            device_id_type=pl.DeviceIdType.MESH,
        )

    mine = pl.ds(pl.multiple_of(core * half, half), half)
    other = pl.ds(pl.multiple_of((1 - core) * half, half), half)
    my_rows = pl.ds(pl.multiple_of(core * rows_dev, rows_dev), rows_dev)
    low, high = pl.ds(0, quarter), pl.ds(quarter, quarter)

    fixed = [
        remote("flux", 0, flux.at[:, other], gath.at[z, y, x, my_rows, :], partner),
        remote("foot", 0, foot.at[:, other], foot_all.at[1], partner),
    ]
    pairs = (
        (owner, owner_p), (tile, tile_p), (lag, lag_p), (sounding, sounding_p),
        (swin, swin_p), (observed, observed_p), (weight, weight_p),
    )
    for at, (src, dst) in enumerate(pairs):
        fixed.append(remote(f"m{at}", 0, src, dst, partner))
    local_flux = pltpu.make_async_copy(flux.at[:, mine], gath.at[z, y, x, my_rows, :], local_sem.at[0])
    local_foot = pltpu.make_async_copy(foot.at[:, mine], foot_all.at[0], local_sem.at[1])
    local_flux.start()
    for copy in fixed:
        copy.start()
    local_foot.start()

    def nearest(k):
        picked = z
        for place in range(depth):
            order = sorted(range(depth), key=lambda other_z: (abs(other_z - place), other_z))
            picked = jnp.where(z == place, order[k], picked)
        return picked

    def gather_z(zz, upward):
        block = gath.at[zz, y, x]
        return remote("gup" if upward else "gdown", zz, block, block, zu if upward else zd)

    def gather_1x(zz):
        block = gath.at[zz, y, x, :, low]
        return remote("g1x", zz, block, block, xn)

    def gather_1y(zz):
        block = gath.at[zz, y, x, :, high]
        return remote("g1y", zz, block, block, yn)

    def gather_2x(zz):
        block = gath.at[zz, :, x, :, high]
        return remote("g2x", zz, block, block, xn)

    def gather_2y(zz):
        block = gath.at[zz, y, :, :, low]
        return remote("g2y", zz, block, block, yn)

    def fields(refs):
        owner_r, tile_r, lag_r, sounding_r, swin_r, _, _ = refs
        count = swin_r.shape[1]
        hot = lax.broadcasted_iota(jnp.int32, (count, entries), 0) == sounding_r[...]
        window = jnp.sum(
            jnp.where(hot, to_col(swin_r[...].astype(jnp.float32)), 0.0), axis=0, keepdims=True
        ) - lag_r[...].astype(jnp.float32)
        window = window.astype(jnp.int32)
        own = to_row(owner_r[...].astype(jnp.float32)).astype(jnp.int32)
        late = jnp.where(window >= windows, 1, 0)
        chip = ((own >> 2) * 2 + late) * 2 + ((own >> 1) & 1)
        inner = (own & 1) * rows_dev + (window - late * windows) * tile_dev + tile_r[...]
        return hot, chip * rows_chip + inner

    sets = (
        (owner, tile, lag, sounding, swin, observed, weight),
        (owner_p, tile_p, lag_p, sounding_p, swin_p, observed_p, weight_p),
    )
    hots, ids = [None, None], [None, None]
    hots[0], ids[0] = fields(sets[0])

    local_flux.wait()
    fixed[0].wait_recv()
    total = [jnp.zeros((entries, 1), jnp.float32)] * 2
    id_cols = [None, None]
    for k in range(depth + 2):
        if k < depth:
            zz = nearest(k)
            if k > 0:
                pl.when(zz < z)(lambda: gather_z(zz, True).wait_recv())
                pl.when(zz > z)(lambda: gather_z(zz, False).wait_recv())
            pl.when((zz <= z) & has_up)(lambda: gather_z(zz, True).start())
            pl.when((zz >= z) & has_down)(lambda: gather_z(zz, False).start())
            gather_1x(zz).start()
            gather_1y(zz).start()
        if k == 1:
            for copy in fixed[1:]:
                copy.wait_recv()
            local_foot.wait()
            hots[1], ids[1] = fields(sets[1])
            id_cols = [to_col(i.astype(jnp.float32)).astype(jnp.int32) for i in ids]
            row_ids[...] = jnp.concatenate(ids, axis=1)
        if 1 <= k <= depth:
            zz = nearest(k - 1)
            gather_1x(zz).wait_recv()
            gather_1y(zz).wait_recv()
            gather_2x(zz).start()
            gather_2y(zz).start()
        if k >= 2:
            zz = nearest(k - 2)
            gather_2x(zz).wait_recv()
            gather_2y(zz).wait_recv()

            def dots(step, acc):
                cells = pl.ds(pl.multiple_of(step * tile_cells, tile_cells), tile_cells)
                block = gath[zz, :, :, :, cells].reshape(rows_plane, tile_cells)
                return tuple(
                    acc[h]
                    + lax.dot_general(
                        foot_all[h, :, cells], block, (((1,), (1,)), ((), ())),
                        preferred_element_type=jnp.float32,
                    )
                    for h in range(2)
                )

            zero = jnp.zeros((entries, rows_plane), jnp.float32)
            acc = lax.fori_loop(0, half // tile_cells, dots, (zero, zero))
            lanes = lax.broadcasted_iota(jnp.int32, (entries, rows_plane), 1) + zz * rows_plane
            for h in range(2):
                total[h] = total[h] + jnp.sum(
                    jnp.where(id_cols[h] == lanes, acc[h], 0.0), axis=1, keepdims=True
                )

    for h in range(2):
        val_send[h] = to_row(total[h])
    vals = remote("vals", 0, val_send, val_recv, partner)
    vals.start()
    vals.wait_recv()
    for h in range(2):
        value = val_send[h] + val_recv[1 - h]
        modeled = to_row(jnp.sum(jnp.where(hots[h], value, 0.0), axis=1, keepdims=True))
        if h == 0:
            modeled_out[...] = modeled
        residual = sets[h][6][...] * (modeled - sets[h][5][...])
        resid = to_col(
            jnp.sum(jnp.where(hots[h], to_col(residual), 0.0), axis=0, keepdims=True)
        )

        def scale(step, carry):
            cells = pl.ds(pl.multiple_of(step * tile_cells, tile_cells), tile_cells)
            scaled = resid * foot_all[h, :, cells].astype(jnp.float32)
            contrib[pl.ds(h * entries, entries), cells] = scaled.astype(jnp.bfloat16)
            return carry

        lax.fori_loop(0, half // tile_cells, scale, 0)

    def partial(rows, cells):
        pick = jnp.where(row_ids[...] == rows, 1.0, 0.0).astype(jnp.bfloat16)
        return jnp.dot(pick, contrib[:, cells], preferred_element_type=jnp.float32)

    def over(offset, body):
        def step_body(step, carry):
            at = pl.multiple_of(step * tile_back, tile_back)
            body(pl.ds(at, tile_back), pl.ds(offset + at, tile_back))
            return carry

        lax.fori_loop(0, quarter // tile_back, step_body, 0)

    def rows_of(zz, yy, xx):
        base = ((zz * 2 + yy) * 2 + xx) * rows_chip
        return lax.broadcasted_iota(jnp.int32, (rows_chip, 2 * entries), 0) + base

    def scatter_1x(zz):
        return remote("s1x", zz, t1x.at[zz], a1x.at[zz], xn)

    def scatter_1y(zz):
        return remote("s1y", zz, t1y.at[zz], a1y.at[zz], yn)

    def scatter_2x(zz):
        return remote("s2x", zz, t2x.at[zz], a2x.at[zz], xn)

    def scatter_2y(zz):
        return remote("s2y", zz, t2y.at[zz], a2y.at[zz], yn)

    def scatter_z(zz, part, upward):
        cells = high if part else low
        kind = ("up" if upward else "down") + str(part)
        into = zup if upward else zdown
        return remote(kind, zz, zsum.at[zz, :, :, cells], into.at[zz, :, :, cells], zu if upward else zd)

    def finish(part, far):
        cells = high if part else low
        into = pl.ds(pl.multiple_of(core * half + part * quarter, quarter), quarter)
        if far:
            return remote("fin", part, zsum.at[z, 1 - core, :, cells], out.at[:, into], partner)
        return pltpu.make_async_copy(zsum.at[z, core, :, cells], out.at[:, into], local_sem.at[part])

    def first(zz):
        row_x = jnp.concatenate([rows_of(zz, 0, 1 - x), rows_of(zz, 1, 1 - x)], axis=0)
        row_y = jnp.concatenate([rows_of(zz, 1 - y, 0), rows_of(zz, 1 - y, 1)], axis=0)

        def for_x(near, cells):
            t1x[zz, :, :, near] = (
                partial(row_x, cells).astype(jnp.bfloat16).reshape(2, rows_chip, tile_back)
            )

        def for_y(near, cells):
            t1y[zz, :, :, near] = (
                partial(row_y, cells).astype(jnp.bfloat16).reshape(2, rows_chip, tile_back)
            )

        over(0, for_x)
        scatter_1x(zz).start()
        over(quarter, for_y)
        scatter_1y(zz).start()

    def second(zz):
        def for_y(near, cells):
            got = a1x[zz, 1 - y, :, near].astype(jnp.float32)
            t2y[zz, :, near] = (partial(rows_of(zz, 1 - y, x), cells) + got).astype(jnp.bfloat16)

        def for_x(near, cells):
            got = a1y[zz, 1 - x, :, near].astype(jnp.float32)
            t2x[zz, :, near] = (partial(rows_of(zz, y, 1 - x), cells) + got).astype(jnp.bfloat16)

        scatter_1x(zz).wait_recv()
        over(0, for_y)
        scatter_2y(zz).start()
        scatter_1y(zz).wait_recv()
        over(quarter, for_x)
        scatter_2x(zz).start()

    def third(zz, part):
        def gather_sum(near, cells):
            if part:
                got = a1y[zz, x, :, near].astype(jnp.float32) + a2x[zz, :, near].astype(jnp.float32)
            else:
                got = a1x[zz, y, :, near].astype(jnp.float32) + a2y[zz, :, near].astype(jnp.float32)
            summed = partial(rows_of(zz, y, x), cells) + got
            zsum[zz, :, :, cells] = summed.reshape(2, rows_dev, tile_back)

        def add_from(source):
            def body(near, cells):
                zsum[zz, :, :, cells] = zsum[zz, :, :, cells] + source[zz, :, :, cells]

            return body

        (scatter_2x if part else scatter_2y)(zz).wait_recv()
        over(part * quarter, gather_sum)

        @pl.when((zz >= z) & has_down)
        def _():
            scatter_z(zz, part, True).wait_recv()
            over(part * quarter, add_from(zup))

        @pl.when((zz <= z) & has_up)
        def _():
            scatter_z(zz, part, False).wait_recv()
            over(part * quarter, add_from(zdown))

        pl.when(zz > z)(lambda: scatter_z(zz, part, True).start())
        pl.when(zz < z)(lambda: scatter_z(zz, part, False).start())

    for k in range(depth + 2):
        if k < depth:
            first(nearest(depth - 1 - k))
        if 1 <= k <= depth:
            second(nearest(depth - k))
        if k >= 2:
            for part in range(2):
                third(nearest(depth + 1 - k), part)
                if k == depth + 1:
                    finish(part, True).start()
                    finish(part, False).start()
    for part in range(2):
        finish(part, False).wait()
        finish(part, True).wait()
    for copy in fixed:
        copy.wait_send()
    vals.wait_send()

    def drain(zz, carry):
        pl.when((zz <= z) & has_up)(lambda: gather_z(zz, True).wait_send())
        pl.when((zz >= z) & has_down)(lambda: gather_z(zz, False).wait_send())
        for copy in (
            gather_1x, gather_1y, gather_2x, gather_2y,
            scatter_1x, scatter_1y, scatter_2x, scatter_2y,
        ):
            copy(zz).wait_send()
        for part in range(2):
            pl.when(zz > z)(lambda: scatter_z(zz, part, True).wait_send())
            pl.when(zz < z)(lambda: scatter_z(zz, part, False).wait_send())
        return carry

    lax.fori_loop(0, depth, drain, 0)


def per_chip(depth, flux, footprint, owner, tile, lag, sounding, swin, observed, weight):
    windows, tile_dev, cells = flux.shape
    entries = footprint.shape[0]
    rows_dev = windows * tile_dev
    rows_chip = 2 * rows_dev
    half, quarter = cells // 2, cells // 4
    sounds = observed.shape[1]
    bf, f32, i32 = jnp.bfloat16, jnp.float32, jnp.int32
    vmem, hbm = pl.BlockSpec(memory_space=pltpu.VMEM), pl.BlockSpec(memory_space=pl.ANY)
    modeled, gradient = pl.pallas_call(
        functools.partial(chip_kernel, depth, windows, tile_dev),
        out_shape=(
            jax.ShapeDtypeStruct((1, sounds), f32),
            jax.ShapeDtypeStruct((rows_dev, cells), f32),
        ),
        in_specs=[hbm, hbm] + [vmem] * 7,
        out_specs=(vmem, vmem),
        scratch_shapes=[
            pltpu.VMEM((2, entries, half), bf),
            pltpu.VMEM((2 * entries, half), bf),
            pltpu.VMEM((depth, 2, 2, rows_chip, half), bf),
            pltpu.VMEM((entries, 1), i32),
            pltpu.VMEM((1, entries), i32),
            pltpu.VMEM((1, entries), i32),
            pltpu.VMEM((1, entries), i32),
            pltpu.VMEM((1, sounds), i32),
            pltpu.VMEM((1, sounds), f32),
            pltpu.VMEM((1, sounds), f32),
            pltpu.VMEM((2, 1, entries), f32),
            pltpu.VMEM((2, 1, entries), f32),
            pltpu.VMEM((1, 2 * entries), i32),
            *[pltpu.VMEM((depth, 2, rows_chip, quarter), bf)] * 4,
            *[pltpu.VMEM((depth, rows_chip, quarter), bf)] * 4,
            *[pltpu.VMEM((depth, 2, rows_dev, half), f32)] * 3,
            pltpu.SemaphoreType.DMA((len(KINDS), depth)),
            pltpu.SemaphoreType.DMA((len(KINDS), depth)),
            pltpu.SemaphoreType.DMA((2,)),
        ],
        compiler_params=pltpu.CompilerParams(collective_id=0, has_side_effects=True),
    )(flux.reshape(rows_dev, cells), footprint, owner, tile, lag, sounding, swin, observed, weight)
    return modeled, gradient.reshape(windows, tile_dev, cells)


def solution(mesh):
    placed = (
        P("tm", "obs", None),
        P(("tm", "obs"), None),
        P(("tm", "obs"), None),
        P(("tm", "obs"), None),
        P(("tm", "obs"), None),
        P(("tm", "obs"), None),
        P(("tm", "obs"), None),
        P(("tm", "obs"), None),
        P(("tm", "obs"), None),
    )
    times, places = mesh.shape["tm"], mesh.shape["obs"]
    depth = places // 4
    grouped = times == 2 and places % 4 == 0 and depth >= 2

    def routed(flux, *rest):
        rows = flux.shape[0] * flux.shape[1] * times * places
        fits = rows * flux.shape[2] * 8 <= 40 * 2**20
        plain = flux.shape[0] * flux.shape[1] % 8 == 0 and flux.shape[2] % 2048 == 0
        body = functools.partial(per_chip, depth) if grouped and fits and plain else per_device
        return body(flux, *rest)

    return jax.shard_map(
        routed,
        mesh=mesh,
        in_specs=placed,
        out_specs=(P(("tm", "obs"), None), P("tm", "obs", None)),
        check_vma=False,
    )
```

```python
import functools

import jax
import jax.numpy as jnp
from jax import lax
from jax.experimental import pallas as pl
from jax.experimental.pallas import tpu as pltpu
from jax.sharding import PartitionSpec as P


def per_device(
    flux,
    footprint,
    entry_owner,
    entry_tile,
    entry_lag,
    entry_sounding,
    sounding_window,
    observed,
    obs_weight,
):
    peer_count = lax.axis_size("obs")
    entry_count = footprint.shape[0]
    cell_count = footprint.shape[1]
    tile_dev = flux.shape[1]
    sounding_count = observed.shape[1]
    slot_cap = 2 * entry_count // peer_count
    owners = entry_owner[:, 0]
    sounding = entry_sounding[0]
    sounding_hot = sounding[:, None] == jnp.arange(sounding_count, dtype=jnp.int32)[None, :]
    window = jnp.sum(jnp.where(sounding_hot, sounding_window[0][None, :], 0), axis=1) - entry_lag[0]
    target = window * tile_dev + entry_tile[0]
    owner_hot = (owners[:, None] == jnp.arange(peer_count, dtype=jnp.int32)[None, :]).astype(
        jnp.int32
    )
    rank_within = jnp.sum((jnp.cumsum(owner_hot, axis=0) - owner_hot) * owner_hot, axis=1)
    slot_index = owners * slot_cap + rank_within
    send_blocks = (
        jnp.zeros((peer_count * slot_cap, cell_count), jnp.bfloat16).at[slot_index].set(footprint)
    )
    send_blocks = send_blocks.reshape(peer_count, slot_cap, cell_count)
    send_target = jnp.zeros((peer_count * slot_cap,), jnp.int32).at[slot_index].set(target)
    send_target = send_target.reshape(peer_count, slot_cap)
    everything = lax.all_gather(flux, "tm", axis=0, tiled=True).reshape(-1, cell_count)
    got_blocks, got_target = (
        lax.all_to_all(send_blocks, "obs", split_axis=0, concat_axis=0, tiled=True),
        lax.all_to_all(send_target, "obs", split_axis=0, concat_axis=0, tiled=True),
    )
    selected = everything[got_target.reshape(-1)].reshape(got_blocks.shape)
    returned = lax.all_to_all(
        jnp.einsum("pkc,pkc->pk", got_blocks, selected, preferred_element_type=jnp.float32),
        "obs",
        split_axis=0,
        concat_axis=0,
        tiled=True,
    )
    entry_dots = returned.reshape(-1)[slot_index]
    modeled = jnp.sum(jnp.where(sounding_hot, entry_dots[:, None], 0.0), axis=0)
    residual = obs_weight[0] * (modeled - observed[0])
    entry_resid = jnp.sum(jnp.where(sounding_hot, residual[None, :], 0.0), axis=1)
    slot_resid = jnp.zeros((peer_count * slot_cap,), jnp.float32).at[slot_index].set(entry_resid)
    got_resid = lax.all_to_all(
        slot_resid.reshape(peer_count, slot_cap), "obs", split_axis=0, concat_axis=0, tiled=True
    )
    contribution = (got_resid[:, :, None] * got_blocks).astype(jnp.bfloat16)
    targets = got_target
    contribution = contribution.reshape(-1, cell_count)
    targets = targets.reshape(-1)
    row_count = flux.shape[0] * lax.axis_size("tm")
    row_ids = jnp.arange(row_count * tile_dev, dtype=jnp.int32)
    row_match = (row_ids[:, None] == targets[None, :]).astype(jnp.bfloat16)
    summed = jnp.dot(row_match, contribution, preferred_element_type=jnp.float32)
    gradient = lax.psum_scatter(
        summed.reshape(row_count, tile_dev * cell_count), "tm", scatter_dimension=0, tiled=True
    )
    gradient = gradient.reshape(flux.shape[0], tile_dev, cell_count)
    return (modeled[None, :], gradient)


KINDS = (
    "foot", "flux", "m0", "m1", "m2", "m3", "m4", "m5", "m6", "vals",
    "gup", "gdown", "g1x", "g1y", "g2x", "g2y",
    "s1x", "s1y", "s2x", "s2y", "z0", "z1", "fin",
)
KIND = {name: at for at, name in enumerate(KINDS)}


def eye(n):
    return lax.broadcasted_iota(jnp.int32, (n, n), 0) == lax.broadcasted_iota(jnp.int32, (n, n), 1)


def to_col(row):
    return jnp.sum(jnp.where(eye(row.shape[1]), row, 0.0), axis=1, keepdims=True)


def to_row(col):
    return jnp.sum(jnp.where(eye(col.shape[0]), col, 0.0), axis=0, keepdims=True)


def chip_kernel(
    depth, windows, tile_dev, flux, foot, owner, tile, lag, sounding, swin, observed, weight,
    modeled_out, out,
    foot_all, contrib, gath, owner_p, tile_p, lag_p, sounding_p, swin_p, observed_p, weight_p,
    val_send, val_recv, row_ids, staged, t1x, t1y, a1x, a1y, t2x, t2y, a2x, a2y, keep_x, keep_y, tz, az, zsum,
    send_sem, recv_sem, local_sem,
):
    entries = foot.shape[0]
    half = foot.shape[1] // 2
    quarter = half // 2
    rows_dev = windows * tile_dev
    rows_chip = 2 * rows_dev
    rows_plane = 4 * rows_chip
    tile_cells = min(1024, quarter)
    tile_back = min(1024, quarter)
    y = lax.axis_index("tm")
    o = lax.axis_index("obs")
    core = lax.rem(o, 2)
    x = lax.rem(o // 2, 2)
    z = o // 4
    partner = (y, o + 1 - 2 * core)
    xn = (y, o + 2 - 4 * x)
    yn = (1 - y, o)
    zu = (y, o + 4)
    zd = (y, o - 4)
    has_up = z < depth - 1
    has_down = z > 0

    def nearest(k):
        picked = z
        for place in range(depth):
            order = sorted(range(depth), key=lambda other_z: (abs(other_z - place), other_z))
            picked = jnp.where(z == place, order[k], picked)
        return picked

    def along_z(zz):
        return (y, o + 4 * (zz - z))

    barrier = pltpu.get_barrier_semaphore()
    for device in (partner, xn, yn, *(along_z(nearest(k)) for k in range(1, depth))):
        pl.semaphore_signal(
            barrier, inc=1, device_id=device, device_id_type=pl.DeviceIdType.MESH
        )
    pl.semaphore_wait(barrier, 2 + depth)

    def remote(kind, at, src, dst, device):
        return pltpu.make_async_remote_copy(
            src_ref=src,
            dst_ref=dst,
            send_sem=send_sem.at[KIND[kind], at],
            recv_sem=recv_sem.at[KIND[kind], at],
            device_id=device,
            device_id_type=pl.DeviceIdType.MESH,
        )

    mine = pl.ds(pl.multiple_of(core * half, half), half)
    other = pl.ds(pl.multiple_of((1 - core) * half, half), half)
    low, high = pl.ds(0, quarter), pl.ds(quarter, quarter)

    fixed = [
        remote("flux", 0, flux.at[:, :, other], staged.at[1], partner),
        remote("foot", 0, foot.at[:, other], foot_all.at[1], partner),
    ]
    pairs = (
        (owner, owner_p), (tile, tile_p), (lag, lag_p), (sounding, sounding_p),
        (swin, swin_p), (observed, observed_p), (weight, weight_p),
    )
    for at, (src, dst) in enumerate(pairs):
        fixed.append(remote(f"m{at}", 0, src, dst, partner))
    local_flux = pltpu.make_async_copy(flux.at[:, :, mine], staged.at[0], local_sem.at[0])
    local_foot = pltpu.make_async_copy(foot.at[:, mine], foot_all.at[0], local_sem.at[1])
    local_flux.start()
    for copy in fixed:
        copy.start()
    local_foot.start()

    def gather_z(zz, upward):
        block = gath.at[zz, y, x]
        return remote("gup" if upward else "gdown", zz, block, block, zu if upward else zd)

    def gather_1x(zz):
        block = gath.at[zz, y, x, :, low]
        return remote("g1x", zz, block, block, xn)

    def gather_1y(zz):
        block = gath.at[zz, y, x, :, high]
        return remote("g1y", zz, block, block, yn)

    def gather_2x(zz):
        block = gath.at[zz, :, x, :, high]
        return remote("g2x", zz, block, block, xn)

    def gather_2y(zz):
        block = gath.at[zz, y, :, :, low]
        return remote("g2y", zz, block, block, yn)

    def fields(refs):
        owner_r, tile_r, lag_r, sounding_r, swin_r, _, _ = refs
        count = swin_r.shape[1]
        hot = lax.broadcasted_iota(jnp.int32, (count, entries), 0) == sounding_r[...]
        window = jnp.sum(
            jnp.where(hot, to_col(swin_r[...].astype(jnp.float32)), 0.0), axis=0, keepdims=True
        ) - lag_r[...].astype(jnp.float32)
        window = window.astype(jnp.int32)
        own = owner_r[...]
        late = jnp.where(window >= windows, 1, 0)
        chip = ((own >> 2) * 2 + late) * 2 + ((own >> 1) & 1)
        inner = (own & 1) * rows_dev + (window - late * windows) * tile_dev + tile_r[...]
        return hot, chip * rows_chip + inner

    sets = (
        (owner, tile, lag, sounding, swin, observed, weight),
        (owner_p, tile_p, lag_p, sounding_p, swin_p, observed_p, weight_p),
    )
    hots, ids = [None, None], [None, None]
    hots[0], ids[0] = fields(sets[0])

    local_flux.wait()
    fixed[0].wait_recv()

    def place(step, carry):
        cells = pl.ds(pl.multiple_of(step * tile_cells, tile_cells), tile_cells)
        own_rows = staged[0, :, :, cells].reshape(rows_dev, tile_cells)
        other_rows = staged[1, :, :, cells].reshape(rows_dev, tile_cells)
        gath[z, y, x, :, cells] = jnp.concatenate(
            [jnp.where(core == 0, own_rows, other_rows), jnp.where(core == 0, other_rows, own_rows)],
            axis=0,
        )
        return carry

    lax.fori_loop(0, half // tile_cells, place, 0)
    total = [jnp.zeros((entries, 1), jnp.float32)] * 2
    id_cols = [None, None]
    for k in range(depth + 2):
        if k < depth:
            zz = nearest(k)
            if k > 0:
                pl.when(zz < z)(lambda: gather_z(zz, True).wait_recv())
                pl.when(zz > z)(lambda: gather_z(zz, False).wait_recv())
            pl.when((zz <= z) & has_up)(lambda: gather_z(zz, True).start())
            pl.when((zz >= z) & has_down)(lambda: gather_z(zz, False).start())
            gather_1x(zz).start()
            gather_1y(zz).start()
        if k == 1:
            for copy in fixed[1:]:
                copy.wait_recv()
            local_foot.wait()
            hots[1], ids[1] = fields(sets[1])
            id_cols = [to_col(i.astype(jnp.float32)).astype(jnp.int32) for i in ids]
            row_ids[...] = jnp.concatenate(ids, axis=1)
        if 1 <= k <= depth:
            zz = nearest(k - 1)
            gather_1x(zz).wait_recv()
            gather_1y(zz).wait_recv()
            gather_2x(zz).start()
            gather_2y(zz).start()
        if k >= 2:
            zz = nearest(k - 2)
            gather_2x(zz).wait_recv()
            gather_2y(zz).wait_recv()

            def dots(step, acc):
                cells = pl.ds(pl.multiple_of(step * tile_cells, tile_cells), tile_cells)
                block = gath[zz, :, :, :, cells].reshape(rows_plane, tile_cells)
                return tuple(
                    acc[h]
                    + lax.dot_general(
                        foot_all[h, :, cells], block, (((1,), (1,)), ((), ())),
                        preferred_element_type=jnp.float32,
                    )
                    for h in range(2)
                )

            zero = jnp.zeros((entries, rows_plane), jnp.float32)
            acc = lax.fori_loop(0, half // tile_cells, dots, (zero, zero))
            lanes = lax.broadcasted_iota(jnp.int32, (entries, rows_plane), 1) + zz * rows_plane
            for h in range(2):
                total[h] = total[h] + jnp.sum(
                    jnp.where(id_cols[h] == lanes, acc[h], 0.0), axis=1, keepdims=True
                )

    for h in range(2):
        val_send[h] = to_row(total[h])
    vals = remote("vals", 0, val_send, val_recv, partner)
    vals.start()
    vals.wait_recv()
    resids = []
    for h in range(2):
        value = val_send[h] + val_recv[1 - h]
        modeled = to_row(jnp.sum(jnp.where(hots[h], value, 0.0), axis=1, keepdims=True))
        if h == 0:
            modeled_out[...] = modeled
        residual = sets[h][6][...] * (modeled - sets[h][5][...])
        resids.append(
            to_col(jnp.sum(jnp.where(hots[h], to_col(residual), 0.0), axis=0, keepdims=True))
        )

    def over(offset, body):
        def step_body(step, carry):
            at = pl.multiple_of(step * tile_back, tile_back)
            body(pl.ds(at, tile_back), pl.ds(offset + at, tile_back))
            return carry

        lax.fori_loop(0, quarter // tile_back, step_body, 0)

    def scale(near, cells):
        for h in range(2):
            scaled = resids[h] * foot_all[h, :, cells].astype(jnp.float32)
            contrib[pl.ds(h * entries, entries), cells] = scaled.astype(jnp.bfloat16)

    def pick_rows(*bases):
        own = lax.broadcasted_iota(jnp.int32, (rows_chip, 2 * entries), 0)
        rows = jnp.concatenate([own + base for base in bases], axis=0)
        return jnp.where(row_ids[...] == rows, 1.0, 0.0).astype(jnp.bfloat16)

    def scatter_1x(zz):
        return remote("s1x", zz, t1x.at[zz], a1x.at[zz], xn)

    def scatter_1y(zz):
        return remote("s1y", zz, t1y.at[zz], a1y.at[zz], yn)

    def scatter_2x(zz):
        return remote("s2x", zz, t2x.at[zz], a2x.at[zz], xn)

    def scatter_2y(zz):
        return remote("s2y", zz, t2y.at[zz], a2y.at[zz], yn)

    def scatter_z(zz, part):
        cells = high if part else low
        kind = KIND[f"z{part}"]
        return pltpu.make_async_remote_copy(
            src_ref=tz.at[zz, :, cells],
            dst_ref=az.at[z, :, cells],
            send_sem=send_sem.at[kind, zz],
            recv_sem=recv_sem.at[kind, z],
            device_id=along_z(zz),
            device_id_type=pl.DeviceIdType.MESH,
        )

    def from_z(zz, part):
        cells = high if part else low
        kind = KIND[f"z{part}"]
        return pltpu.make_async_remote_copy(
            src_ref=tz.at[zz, :, cells],
            dst_ref=az.at[zz, :, cells],
            send_sem=send_sem.at[kind, zz],
            recv_sem=recv_sem.at[kind, zz],
            device_id=along_z(zz),
            device_id_type=pl.DeviceIdType.MESH,
        )

    def finish(part, far):
        cells = high if part else low
        into = pl.ds(pl.multiple_of(core * half + part * quarter, quarter), quarter)
        if far:
            return remote("fin", part, zsum.at[1 - core, :, cells], out.at[:, into], partner)
        return pltpu.make_async_copy(zsum.at[core, :, cells], out.at[:, into], local_sem.at[part])

    def first(zz, fresh):
        def chip(yy, xx):
            return ((zz * 2 + yy) * 2 + xx) * rows_chip

        def run(offset, bases, sent, kept):
            pick = pick_rows(*bases)

            def body(near, cells):
                summed = jnp.dot(pick, contrib[:, cells], preferred_element_type=jnp.float32)
                summed = summed.reshape(2, 2, rows_chip, tile_back)
                sent[zz, :, :, near] = summed[0].astype(jnp.bfloat16)
                kept[zz, :, :, near] = summed[1]

            if fresh:
                over(offset, scale)
            over(offset, body)

        run(0, (chip(0, 1 - x), chip(1, 1 - x), chip(0, x), chip(1, x)), t1x, keep_x)
        scatter_1x(zz).start()
        run(quarter, (chip(1 - y, 0), chip(1 - y, 1), chip(y, 0), chip(y, 1)), t1y, keep_y)
        scatter_1y(zz).start()

    def second(zz):
        def for_y(near, cells):
            got = a1x[zz, 1 - y, :, near].astype(jnp.float32)
            t2y[zz, :, near] = (keep_x[zz, 1 - y, :, near] + got).astype(jnp.bfloat16)

        def for_x(near, cells):
            got = a1y[zz, 1 - x, :, near].astype(jnp.float32)
            t2x[zz, :, near] = (keep_y[zz, 1 - x, :, near] + got).astype(jnp.bfloat16)

        scatter_1x(zz).wait_recv()
        over(0, for_y)
        scatter_2y(zz).start()
        scatter_1y(zz).wait_recv()
        over(quarter, for_x)
        scatter_2x(zz).start()

    def third(zz, part, last):
        def plane_sum(near):
            if part:
                return keep_y[zz, x, :, near] + (
                    a1y[zz, x, :, near].astype(jnp.float32) + a2x[zz, :, near].astype(jnp.float32)
                )
            return keep_x[zz, y, :, near] + (
                a1x[zz, y, :, near].astype(jnp.float32) + a2y[zz, :, near].astype(jnp.float32)
            )

        def send_on(near, cells):
            tz[zz, :, cells] = plane_sum(near).astype(jnp.bfloat16)

        def sum_up(near, cells):
            summed = plane_sum(near)
            for k in range(1, depth):
                summed = summed + az[nearest(k), :, cells].astype(jnp.float32)
            zsum[:, :, cells] = summed.reshape(2, rows_dev, tile_back)

        (scatter_2x if part else scatter_2y)(zz).wait_recv()
        if last:
            for k in range(1, depth):
                from_z(nearest(k), part).wait_recv()
            over(part * quarter, sum_up)
        else:
            over(part * quarter, send_on)
            scatter_z(zz, part).start()

    for k in range(depth + 2):
        if k < depth:
            first(nearest(depth - 1 - k), k == 0)
        if 1 <= k <= depth:
            second(nearest(depth - k))
        if k >= 2:
            for part in range(2):
                third(nearest(depth + 1 - k), part, k == depth + 1)
                if k == depth + 1:
                    finish(part, True).start()
                    finish(part, False).start()
    for part in range(2):
        finish(part, False).wait()
        finish(part, True).wait()
    for copy in fixed:
        copy.wait_send()
    vals.wait_send()
    for k in range(1, depth):
        for part in range(2):
            scatter_z(nearest(k), part).wait_send()

    def drain(zz, carry):
        pl.when((zz <= z) & has_up)(lambda: gather_z(zz, True).wait_send())
        pl.when((zz >= z) & has_down)(lambda: gather_z(zz, False).wait_send())
        for copy in (
            gather_1x, gather_1y, gather_2x, gather_2y,
            scatter_1x, scatter_1y, scatter_2x, scatter_2y,
        ):
            copy(zz).wait_send()
        return carry

    lax.fori_loop(0, depth, drain, 0)


def per_chip(depth, flux, footprint, owner, tile, lag, sounding, swin, observed, weight):
    windows, tile_dev, cells = flux.shape
    entries = footprint.shape[0]
    rows_dev = windows * tile_dev
    rows_chip = 2 * rows_dev
    half, quarter = cells // 2, cells // 4
    sounds = observed.shape[1]
    bf, f32, i32 = jnp.bfloat16, jnp.float32, jnp.int32
    vmem, hbm = pl.BlockSpec(memory_space=pltpu.VMEM), pl.BlockSpec(memory_space=pl.ANY)
    modeled, gradient = pl.pallas_call(
        functools.partial(chip_kernel, depth, windows, tile_dev),
        out_shape=(
            jax.ShapeDtypeStruct((1, sounds), f32),
            jax.ShapeDtypeStruct((rows_dev, cells), f32),
        ),
        in_specs=[hbm, hbm] + [vmem] * 7,
        out_specs=(vmem, vmem),
        scratch_shapes=[
            pltpu.VMEM((2, entries, half), bf),
            pltpu.VMEM((2 * entries, half), bf),
            pltpu.VMEM((depth, 2, 2, rows_chip, half), bf),
            pltpu.VMEM((1, entries), i32),
            pltpu.VMEM((1, entries), i32),
            pltpu.VMEM((1, entries), i32),
            pltpu.VMEM((1, entries), i32),
            pltpu.VMEM((1, sounds), i32),
            pltpu.VMEM((1, sounds), f32),
            pltpu.VMEM((1, sounds), f32),
            pltpu.VMEM((2, 1, entries), f32),
            pltpu.VMEM((2, 1, entries), f32),
            pltpu.VMEM((1, 2 * entries), i32),
            pltpu.VMEM((2, windows, tile_dev, half), bf),
            *[pltpu.VMEM((depth, 2, rows_chip, quarter), bf)] * 4,
            *[pltpu.VMEM((depth, rows_chip, quarter), bf)] * 4,
            *[pltpu.VMEM((depth, 2, rows_chip, quarter), f32)] * 2,
            *[pltpu.VMEM((depth, rows_chip, half), bf)] * 2,
            pltpu.VMEM((2, rows_dev, half), f32),
            pltpu.SemaphoreType.DMA((len(KINDS), depth)),
            pltpu.SemaphoreType.DMA((len(KINDS), depth)),
            pltpu.SemaphoreType.DMA((2,)),
        ],
        compiler_params=pltpu.CompilerParams(collective_id=0, has_side_effects=True),
    )(flux, footprint, owner.reshape(1, entries), tile, lag, sounding, swin, observed, weight)
    return modeled, gradient.reshape(windows, tile_dev, cells)


def solution(mesh):
    placed = (
        P("tm", "obs", None),
        P(("tm", "obs"), None),
        P(("tm", "obs"), None),
        P(("tm", "obs"), None),
        P(("tm", "obs"), None),
        P(("tm", "obs"), None),
        P(("tm", "obs"), None),
        P(("tm", "obs"), None),
        P(("tm", "obs"), None),
    )
    times, places = mesh.shape["tm"], mesh.shape["obs"]
    depth = places // 4
    grouped = times == 2 and places % 4 == 0 and depth >= 2

    def routed(flux, *rest):
        rows = flux.shape[0] * flux.shape[1] * times * places
        fits = rows * flux.shape[2] * 8 <= 40 * 2**20
        plain = flux.shape[0] * flux.shape[1] % 8 == 0 and flux.shape[2] % 2048 == 0
        body = functools.partial(per_chip, depth) if grouped and fits and plain else per_device
        return body(flux, *rest)

    return jax.shard_map(
        routed,
        mesh=mesh,
        in_specs=placed,
        out_specs=(P(("tm", "obs"), None), P("tm", "obs", None)),
        check_vma=False,
    )
```

```python
import functools

import jax
import jax.numpy as jnp
from jax import lax
from jax.experimental import pallas as pl
from jax.experimental.pallas import tpu as pltpu
from jax.sharding import PartitionSpec as P


def per_device(
    flux,
    footprint,
    entry_owner,
    entry_tile,
    entry_lag,
    entry_sounding,
    sounding_window,
    observed,
    obs_weight,
):
    peer_count = lax.axis_size("obs")
    entry_count = footprint.shape[0]
    cell_count = footprint.shape[1]
    tile_dev = flux.shape[1]
    sounding_count = observed.shape[1]
    slot_cap = 2 * entry_count // peer_count
    owners = entry_owner[:, 0]
    sounding = entry_sounding[0]
    sounding_hot = sounding[:, None] == jnp.arange(sounding_count, dtype=jnp.int32)[None, :]
    window = jnp.sum(jnp.where(sounding_hot, sounding_window[0][None, :], 0), axis=1) - entry_lag[0]
    target = window * tile_dev + entry_tile[0]
    owner_hot = (owners[:, None] == jnp.arange(peer_count, dtype=jnp.int32)[None, :]).astype(
        jnp.int32
    )
    rank_within = jnp.sum((jnp.cumsum(owner_hot, axis=0) - owner_hot) * owner_hot, axis=1)
    slot_index = owners * slot_cap + rank_within
    send_blocks = (
        jnp.zeros((peer_count * slot_cap, cell_count), jnp.bfloat16).at[slot_index].set(footprint)
    )
    send_blocks = send_blocks.reshape(peer_count, slot_cap, cell_count)
    send_target = jnp.zeros((peer_count * slot_cap,), jnp.int32).at[slot_index].set(target)
    send_target = send_target.reshape(peer_count, slot_cap)
    everything = lax.all_gather(flux, "tm", axis=0, tiled=True).reshape(-1, cell_count)
    got_blocks, got_target = (
        lax.all_to_all(send_blocks, "obs", split_axis=0, concat_axis=0, tiled=True),
        lax.all_to_all(send_target, "obs", split_axis=0, concat_axis=0, tiled=True),
    )
    selected = everything[got_target.reshape(-1)].reshape(got_blocks.shape)
    returned = lax.all_to_all(
        jnp.einsum("pkc,pkc->pk", got_blocks, selected, preferred_element_type=jnp.float32),
        "obs",
        split_axis=0,
        concat_axis=0,
        tiled=True,
    )
    entry_dots = returned.reshape(-1)[slot_index]
    modeled = jnp.sum(jnp.where(sounding_hot, entry_dots[:, None], 0.0), axis=0)
    residual = obs_weight[0] * (modeled - observed[0])
    entry_resid = jnp.sum(jnp.where(sounding_hot, residual[None, :], 0.0), axis=1)
    slot_resid = jnp.zeros((peer_count * slot_cap,), jnp.float32).at[slot_index].set(entry_resid)
    got_resid = lax.all_to_all(
        slot_resid.reshape(peer_count, slot_cap), "obs", split_axis=0, concat_axis=0, tiled=True
    )
    contribution = (got_resid[:, :, None] * got_blocks).astype(jnp.bfloat16)
    targets = got_target
    contribution = contribution.reshape(-1, cell_count)
    targets = targets.reshape(-1)
    row_count = flux.shape[0] * lax.axis_size("tm")
    row_ids = jnp.arange(row_count * tile_dev, dtype=jnp.int32)
    row_match = (row_ids[:, None] == targets[None, :]).astype(jnp.bfloat16)
    summed = jnp.dot(row_match, contribution, preferred_element_type=jnp.float32)
    gradient = lax.psum_scatter(
        summed.reshape(row_count, tile_dev * cell_count), "tm", scatter_dimension=0, tiled=True
    )
    gradient = gradient.reshape(flux.shape[0], tile_dev, cell_count)
    return (modeled[None, :], gradient)


KINDS = (
    "foot", "flux", "m0", "m1", "m2", "m3", "m4", "m5", "m6", "vals",
    "gup0", "gup1", "gup2", "gdown0", "gdown1", "gdown2", "g1x", "g1y", "g2x", "g2y",
    "s1x", "s1y", "s2x", "s2y", "z0", "z1", "fin",
)
KIND = {name: at for at, name in enumerate(KINDS)}


def eye(n):
    return lax.broadcasted_iota(jnp.int32, (n, n), 0) == lax.broadcasted_iota(jnp.int32, (n, n), 1)


def to_col(row):
    return jnp.sum(jnp.where(eye(row.shape[1]), row, 0.0), axis=1, keepdims=True)


def to_row(col):
    return jnp.sum(jnp.where(eye(col.shape[0]), col, 0.0), axis=0, keepdims=True)


def chip_kernel(
    depth, windows, tile_dev, flux, foot, owner, tile, lag, sounding, swin, observed, weight,
    modeled_out, out,
    foot_all, contrib, gath, owner_p, tile_p, lag_p, sounding_p, swin_p, observed_p, weight_p,
    val_send, val_recv, row_ids, staged, t1x, t1y, a1x, a1y, t2x, t2y, a2x, a2y, keep_x, keep_y, tz, az, zsum,
    send_sem, recv_sem, local_sem,
):
    entries = foot.shape[0]
    half = foot.shape[1] // 2
    quarter = half // 2
    rows_dev = windows * tile_dev
    rows_chip = 2 * rows_dev
    rows_plane = 4 * rows_chip
    extra = quarter // 2048 * 384
    tile_cells = min(1024, quarter)
    tile_back = min(1024, quarter)
    y = lax.axis_index("tm")
    o = lax.axis_index("obs")
    core = lax.rem(o, 2)
    x = lax.rem(o // 2, 2)
    z = o // 4
    partner = (y, o + 1 - 2 * core)
    xn = (y, o + 2 - 4 * x)
    yn = (1 - y, o)
    zu = (y, o + 4)
    zd = (y, o - 4)
    has_up = z < depth - 1
    has_down = z > 0

    def nearest(k):
        picked = z
        for place in range(depth):
            order = sorted(range(depth), key=lambda other_z: (abs(other_z - place), other_z))
            picked = jnp.where(z == place, order[k], picked)
        return picked

    def along_z(zz):
        return (y, o + 4 * (zz - z))

    mine = pl.ds(pl.multiple_of(core * half, half), half)
    other = pl.ds(pl.multiple_of((1 - core) * half, half), half)
    low, high = pl.ds(0, quarter), pl.ds(quarter, quarter)
    local_flux = pltpu.make_async_copy(flux.at[:, :, mine], staged.at[0], local_sem.at[0])
    local_foot = pltpu.make_async_copy(foot.at[:, mine], foot_all.at[0], local_sem.at[1])
    barrier = pltpu.get_barrier_semaphore()
    for device in (partner, xn, yn, *(along_z(nearest(k)) for k in range(1, depth))):
        pl.semaphore_signal(
            barrier, inc=1, device_id=device, device_id_type=pl.DeviceIdType.MESH
        )
    local_flux.start()
    local_foot.start()
    pl.semaphore_wait(barrier, 2 + depth)

    def remote(kind, at, src, dst, device):
        return pltpu.make_async_remote_copy(
            src_ref=src,
            dst_ref=dst,
            send_sem=send_sem.at[KIND[kind], at],
            recv_sem=recv_sem.at[KIND[kind], at],
            device_id=device,
            device_id_type=pl.DeviceIdType.MESH,
        )

    fixed = [
        remote("flux", 0, flux.at[:, :, other], staged.at[1], partner),
        remote("foot", 0, foot.at[:, other], foot_all.at[1], partner),
    ]
    pairs = (
        (owner, owner_p), (tile, tile_p), (lag, lag_p), (sounding, sounding_p),
        (swin, swin_p), (observed, observed_p), (weight, weight_p),
    )
    for at, (src, dst) in enumerate(pairs):
        fixed.append(remote(f"m{at}", 0, src, dst, partner))
    for copy in fixed:
        copy.start()

    def gather_z(zz, part, upward):
        cells = (
            pl.ds(0, quarter - extra),
            pl.ds(quarter + extra, quarter - extra),
            pl.ds(quarter - extra, 2 * extra),
        )[part]
        block = gath.at[zz, :, :, :, cells] if part == 2 else gath.at[zz, y, x, :, cells]
        kind = ("gup" if upward else "gdown") + str(part)
        return remote(kind, zz, block, block, zu if upward else zd)

    def send_z(zz, parts):
        for part in parts:
            pl.when((zz <= z) & has_up)(lambda: gather_z(zz, part, True).start())
            pl.when((zz >= z) & has_down)(lambda: gather_z(zz, part, False).start())

    def take_z(zz, parts):
        for part in parts:
            pl.when(zz < z)(lambda: gather_z(zz, part, True).wait_recv())
            pl.when(zz > z)(lambda: gather_z(zz, part, False).wait_recv())

    def low_of(own):
        return low if own else pl.ds(0, quarter - extra)

    def high_of(own):
        return high if own else pl.ds(quarter + extra, quarter - extra)

    def gather_1x(zz, own):
        block = gath.at[zz, y, x, :, low_of(own)]
        return remote("g1x", zz, block, block, xn)

    def gather_1y(zz, own):
        block = gath.at[zz, y, x, :, high_of(own)]
        return remote("g1y", zz, block, block, yn)

    def gather_2x(zz, own):
        block = gath.at[zz, :, x, :, high_of(own)]
        return remote("g2x", zz, block, block, xn)

    def gather_2y(zz, own):
        block = gath.at[zz, y, :, :, low_of(own)]
        return remote("g2y", zz, block, block, yn)

    def fields(refs):
        owner_r, tile_r, lag_r, sounding_r, swin_r, _, _ = refs
        count = swin_r.shape[1]
        hot = lax.broadcasted_iota(jnp.int32, (count, entries), 0) == sounding_r[...]
        window = jnp.sum(
            jnp.where(hot, to_col(swin_r[...].astype(jnp.float32)), 0.0), axis=0, keepdims=True
        ) - lag_r[...].astype(jnp.float32)
        window = window.astype(jnp.int32)
        own = owner_r[...]
        late = jnp.where(window >= windows, 1, 0)
        chip = ((own >> 2) * 2 + late) * 2 + ((own >> 1) & 1)
        inner = (own & 1) * rows_dev + (window - late * windows) * tile_dev + tile_r[...]
        return hot, chip * rows_chip + inner

    sets = (
        (owner, tile, lag, sounding, swin, observed, weight),
        (owner_p, tile_p, lag_p, sounding_p, swin_p, observed_p, weight_p),
    )
    hots, ids = [None, None], [None, None]
    hots[0], ids[0] = fields(sets[0])

    local_flux.wait()
    fixed[0].wait_recv()

    def place(step, carry):
        cells = pl.ds(pl.multiple_of(step * tile_cells, tile_cells), tile_cells)
        own_rows = staged[0, :, :, cells].reshape(rows_dev, tile_cells)
        other_rows = staged[1, :, :, cells].reshape(rows_dev, tile_cells)
        gath[z, y, x, :, cells] = jnp.concatenate(
            [jnp.where(core == 0, own_rows, other_rows), jnp.where(core == 0, other_rows, own_rows)],
            axis=0,
        )
        return carry

    lax.fori_loop(0, half // tile_cells, place, 0)
    def arrive(k):
        zz = nearest(k)
        if k > 0:
            take_z(zz, (0, 1))
        send_z(zz, (0, 1))
        gather_1x(zz, k == 0).start()
        gather_1y(zz, k == 0).start()

    def widen(k):
        zz = nearest(k)
        gather_1x(zz, k == 0).wait_recv()
        gather_1y(zz, k == 0).wait_recv()
        gather_2x(zz, k == 0).start()
        gather_2y(zz, k == 0).start()

    def complete(k):
        zz = nearest(k)
        gather_2x(zz, k == 0).wait_recv()
        gather_2y(zz, k == 0).wait_recv()

    def spread(k):
        zz = nearest(k)
        if k > 0:
            take_z(zz, (2,))
        send_z(zz, (2,))

    def values(k, total, ids_col):
        zz = nearest(k)

        def dots(step, acc):
            cells = pl.ds(pl.multiple_of(step * quarter, quarter), quarter)
            return acc + lax.dot_general(
                foot_all[:, :, cells].reshape(2 * entries, quarter),
                gath[zz, :, :, :, cells].reshape(rows_plane, quarter),
                (((1,), (1,)), ((), ())),
                preferred_element_type=jnp.float32,
            )

        acc = lax.fori_loop(
            0, half // quarter, dots, jnp.zeros((2 * entries, rows_plane), jnp.float32)
        )
        lanes = lax.broadcasted_iota(jnp.int32, (2 * entries, rows_plane), 1) + zz * rows_plane
        return total + jnp.sum(jnp.where(ids_col == lanes, acc, 0.0), axis=1, keepdims=True)

    arrive(0)
    widen(0)
    total = jnp.zeros((2 * entries, 1), jnp.float32)
    arrive(1)
    complete(0)
    spread(0)
    for copy in fixed[1:]:
        copy.wait_recv()
    local_foot.wait()
    hots[1], ids[1] = fields(sets[1])
    row_ids[...] = jnp.concatenate(ids, axis=1)
    ids_col = jnp.concatenate(
        [to_col(i.astype(jnp.float32)).astype(jnp.int32) for i in ids], axis=0
    )
    total = values(0, total, ids_col)
    for k in range(2, depth):
        arrive(k)
        if k < depth - 1:
            widen(k - 1)
    widen(max(depth - 2, 1))
    if depth > 2:
        widen(depth - 1)
    spread(1)
    if depth > 2:
        spread(2)
    for k in range(1, depth):
        complete(k)
        if k > 2:
            spread(k)
        total = values(k, total, ids_col)

    for h in range(2):
        val_send[h] = to_row(total[h * entries : (h + 1) * entries])
    vals = remote("vals", 0, val_send, val_recv, partner)
    vals.start()
    vals.wait_recv()
    resids = []
    for h in range(2):
        value = val_send[h] + val_recv[1 - h]
        modeled = to_row(jnp.sum(jnp.where(hots[h], value, 0.0), axis=1, keepdims=True))
        if h == 0:
            modeled_out[...] = modeled
        residual = sets[h][6][...] * (modeled - sets[h][5][...])
        resids.append(
            to_col(jnp.sum(jnp.where(hots[h], to_col(residual), 0.0), axis=0, keepdims=True))
        )

    def over(offset, body):
        def step_body(step, carry):
            at = pl.multiple_of(step * tile_back, tile_back)
            body(pl.ds(at, tile_back), pl.ds(offset + at, tile_back))
            return carry

        lax.fori_loop(0, quarter // tile_back, step_body, 0)

    def scale(near, cells):
        for h in range(2):
            scaled = resids[h] * foot_all[h, :, cells].astype(jnp.float32)
            contrib[pl.ds(h * entries, entries), cells] = scaled.astype(jnp.bfloat16)

    def pick_rows(*bases):
        own = lax.broadcasted_iota(jnp.int32, (rows_chip, 2 * entries), 0)
        rows = jnp.concatenate([own + base for base in bases], axis=0)
        return jnp.where(row_ids[...] == rows, 1.0, 0.0).astype(jnp.bfloat16)

    def scatter_1x(zz):
        return remote("s1x", zz, t1x.at[zz], a1x.at[zz], xn)

    def scatter_1y(zz):
        return remote("s1y", zz, t1y.at[zz], a1y.at[zz], yn)

    def scatter_2x(zz):
        return remote("s2x", zz, t2x.at[zz], a2x.at[zz], xn)

    def scatter_2y(zz):
        return remote("s2y", zz, t2y.at[zz], a2y.at[zz], yn)

    def scatter_z(zz, part):
        cells = high if part else low
        kind = KIND[f"z{part}"]
        return pltpu.make_async_remote_copy(
            src_ref=tz.at[zz, :, cells],
            dst_ref=az.at[z, :, cells],
            send_sem=send_sem.at[kind, zz],
            recv_sem=recv_sem.at[kind, z],
            device_id=along_z(zz),
            device_id_type=pl.DeviceIdType.MESH,
        )

    def from_z(zz, part):
        cells = high if part else low
        kind = KIND[f"z{part}"]
        return pltpu.make_async_remote_copy(
            src_ref=tz.at[zz, :, cells],
            dst_ref=az.at[zz, :, cells],
            send_sem=send_sem.at[kind, zz],
            recv_sem=recv_sem.at[kind, zz],
            device_id=along_z(zz),
            device_id_type=pl.DeviceIdType.MESH,
        )

    def finish(part, far):
        cells = high if part else low
        into = pl.ds(pl.multiple_of(core * half + part * quarter, quarter), quarter)
        if far:
            return remote("fin", part, zsum.at[1 - core, :, cells], out.at[:, into], partner)
        return pltpu.make_async_copy(zsum.at[core, :, cells], out.at[:, into], local_sem.at[part])

    def first(zz, fresh):
        def chip(yy, xx):
            return ((zz * 2 + yy) * 2 + xx) * rows_chip

        def run(offset, bases, sent, kept):
            pick = pick_rows(*bases)

            def body(near, cells):
                summed = jnp.dot(pick, contrib[:, cells], preferred_element_type=jnp.float32)
                summed = summed.reshape(2, 2, rows_chip, tile_back)
                sent[zz, :, :, near] = summed[0].astype(jnp.bfloat16)
                kept[zz, :, :, near] = summed[1]

            if fresh:
                over(offset, scale)
            over(offset, body)

        run(0, (chip(0, 1 - x), chip(1, 1 - x), chip(0, x), chip(1, x)), t1x, keep_x)
        scatter_1x(zz).start()
        run(quarter, (chip(1 - y, 0), chip(1 - y, 1), chip(y, 0), chip(y, 1)), t1y, keep_y)
        scatter_1y(zz).start()

    def second(zz):
        def for_y(near, cells):
            got = a1x[zz, 1 - y, :, near].astype(jnp.float32)
            t2y[zz, :, near] = (keep_x[zz, 1 - y, :, near] + got).astype(jnp.bfloat16)

        def for_x(near, cells):
            got = a1y[zz, 1 - x, :, near].astype(jnp.float32)
            t2x[zz, :, near] = (keep_y[zz, 1 - x, :, near] + got).astype(jnp.bfloat16)

        scatter_1x(zz).wait_recv()
        over(0, for_y)
        scatter_2y(zz).start()
        scatter_1y(zz).wait_recv()
        over(quarter, for_x)
        scatter_2x(zz).start()

    def third(zz, part, last):
        def plane_sum(near):
            if part:
                return keep_y[zz, x, :, near] + (
                    a1y[zz, x, :, near].astype(jnp.float32) + a2x[zz, :, near].astype(jnp.float32)
                )
            return keep_x[zz, y, :, near] + (
                a1x[zz, y, :, near].astype(jnp.float32) + a2y[zz, :, near].astype(jnp.float32)
            )

        def send_on(near, cells):
            tz[zz, :, cells] = plane_sum(near).astype(jnp.bfloat16)

        def sum_up(near, cells):
            summed = plane_sum(near)
            for k in range(1, depth):
                summed = summed + az[nearest(k), :, cells].astype(jnp.float32)
            zsum[:, :, cells] = summed.reshape(2, rows_dev, tile_back)

        (scatter_2x if part else scatter_2y)(zz).wait_recv()
        if last:
            for k in range(1, depth):
                from_z(nearest(k), part).wait_recv()
            over(part * quarter, sum_up)
        else:
            over(part * quarter, send_on)
            scatter_z(zz, part).start()

    def leave(k):
        for part in range(2):
            third(nearest(depth - 1 - k), part, k == depth - 1)
            if k == depth - 1:
                finish(part, True).start()
                finish(part, False).start()

    for k in range(depth - 1):
        first(nearest(depth - 1 - k), k == 0)
        if k > 0:
            second(nearest(depth - k))
        if k > 1:
            leave(k - 2)
    second(nearest(1))
    first(nearest(0), False)
    for k in range(max(depth - 3, 0), depth - 1):
        leave(k)
    second(nearest(0))
    leave(depth - 1)
    for part in range(2):
        finish(part, False).wait()
        finish(part, True).wait()
    for copy in fixed:
        copy.wait_send()
    vals.wait_send()
    for k in range(1, depth):
        for part in range(2):
            scatter_z(nearest(k), part).wait_send()

    def drain(zz, carry):
        for part in range(3):
            pl.when((zz <= z) & has_up)(lambda: gather_z(zz, part, True).wait_send())
            pl.when((zz >= z) & has_down)(lambda: gather_z(zz, part, False).wait_send())
        for copy in (scatter_1x, scatter_1y, scatter_2x, scatter_2y):
            copy(zz).wait_send()
        return carry

    lax.fori_loop(0, depth, drain, 0)
    for k in range(depth):
        for copy in (gather_1x, gather_1y, gather_2x, gather_2y):
            copy(nearest(k), k == 0).wait_send()


def per_chip(depth, flux, footprint, owner, tile, lag, sounding, swin, observed, weight):
    windows, tile_dev, cells = flux.shape
    entries = footprint.shape[0]
    rows_dev = windows * tile_dev
    rows_chip = 2 * rows_dev
    half, quarter = cells // 2, cells // 4
    sounds = observed.shape[1]
    bf, f32, i32 = jnp.bfloat16, jnp.float32, jnp.int32
    vmem, hbm = pl.BlockSpec(memory_space=pltpu.VMEM), pl.BlockSpec(memory_space=pl.ANY)
    modeled, gradient = pl.pallas_call(
        functools.partial(chip_kernel, depth, windows, tile_dev),
        out_shape=(
            jax.ShapeDtypeStruct((1, sounds), f32),
            jax.ShapeDtypeStruct((rows_dev, cells), f32),
        ),
        in_specs=[hbm, hbm] + [vmem] * 7,
        out_specs=(vmem, vmem),
        scratch_shapes=[
            pltpu.VMEM((2, entries, half), bf),
            pltpu.VMEM((2 * entries, half), bf),
            pltpu.VMEM((depth, 2, 2, rows_chip, half), bf),
            pltpu.VMEM((1, entries), i32),
            pltpu.VMEM((1, entries), i32),
            pltpu.VMEM((1, entries), i32),
            pltpu.VMEM((1, entries), i32),
            pltpu.VMEM((1, sounds), i32),
            pltpu.VMEM((1, sounds), f32),
            pltpu.VMEM((1, sounds), f32),
            pltpu.VMEM((2, 1, entries), f32),
            pltpu.VMEM((2, 1, entries), f32),
            pltpu.VMEM((1, 2 * entries), i32),
            pltpu.VMEM((2, windows, tile_dev, half), bf),
            *[pltpu.VMEM((depth, 2, rows_chip, quarter), bf)] * 4,
            *[pltpu.VMEM((depth, rows_chip, quarter), bf)] * 4,
            *[pltpu.VMEM((depth, 2, rows_chip, quarter), f32)] * 2,
            *[pltpu.VMEM((depth, rows_chip, half), bf)] * 2,
            pltpu.VMEM((2, rows_dev, half), f32),
            pltpu.SemaphoreType.DMA((len(KINDS), depth)),
            pltpu.SemaphoreType.DMA((len(KINDS), depth)),
            pltpu.SemaphoreType.DMA((2,)),
        ],
        compiler_params=pltpu.CompilerParams(collective_id=0, has_side_effects=True),
    )(flux, footprint, owner.reshape(1, entries), tile, lag, sounding, swin, observed, weight)
    return modeled, gradient.reshape(windows, tile_dev, cells)


def solution(mesh):
    placed = (
        P("tm", "obs", None),
        P(("tm", "obs"), None),
        P(("tm", "obs"), None),
        P(("tm", "obs"), None),
        P(("tm", "obs"), None),
        P(("tm", "obs"), None),
        P(("tm", "obs"), None),
        P(("tm", "obs"), None),
        P(("tm", "obs"), None),
    )
    times, places = mesh.shape["tm"], mesh.shape["obs"]
    depth = places // 4
    grouped = times == 2 and places % 4 == 0 and depth >= 2

    def routed(flux, *rest):
        rows = flux.shape[0] * flux.shape[1] * times * places
        fits = rows * flux.shape[2] * 8 <= 40 * 2**20
        plain = flux.shape[0] * flux.shape[1] % 8 == 0 and flux.shape[2] % 8192 == 0
        body = functools.partial(per_chip, depth) if grouped and fits and plain else per_device
        return body(flux, *rest)

    return jax.shard_map(
        routed,
        mesh=mesh,
        in_specs=placed,
        out_specs=(P(("tm", "obs"), None), P("tm", "obs", None)),
        check_vma=False,
    )
```
